512 devices in a mesh: row: 32 (over x, y, core), col: 16 (over z).
Axes of the slice: x: 4, y: 4, z: 16, core: 2. Of those that a mesh axis runs over, the one named last changes fastest.
Arguments:
- tokens: bfloat16 [256, 8192], P('row', 'col'), may hold values from -6 to 6
- gate_blocks: bfloat16 [16, 32, 10, 128, 128], P('col', 'row'), may hold values from -0.1875 to 0.1875
- up_blocks: bfloat16 [16, 32, 10, 128, 128], P('col', 'row'), may hold values from -0.1875 to 0.1875
- down_blocks: bfloat16 [32, 16, 10, 128, 128], P('row', 'col'), may hold values from -0.09375 to 0.09375
- gate_slots: int32 [16, 32, 10], P('col', 'row'), may hold values from 0 to 32, as said below
- up_slots: int32 [16, 32, 10], P('col', 'row'), may hold values from 0 to 32, as said below
- down_slots: int32 [32, 16, 10], P('row', 'col'), may hold values from 0 to 32, as said below
- out_grad: bfloat16 [256, 8192], P('row', 'col'), may hold values from -6 to 6
Outputs:
- layer_out: bfloat16 [256, 8192], P('row', 'col')
- token_grad: bfloat16 [256, 8192], P('row', 'col')
- gate_grad: float32 [16, 32, 10, 128, 128], P('col', 'row')
- up_grad: float32 [16, 32, 10, 128, 128], P('col', 'row')
- down_grad: float32 [32, 16, 10, 128, 128], P('row', 'col')
The draws below stay inside these ranges and needn't reach their ends.
Inputs may be any that keep to these rules, and one draw needn't show every extreme that they name: `gate_slots`: in every tile the live slots come first and hold distinct block numbers below 32; the other slots hold 32 and are empty; every tile has a live slot, and some tile has all 10 live. `up_slots`: as for gate_slots. `down_slots`: as for gate_slots, with numbers b naming block row b // 4 and block column b % 4 of a tile.
All inputs are finite; a program needn't handle non-finite values.
Results may differ from the reference program's by a relative error of at most 0.025.
Values may be sent and summed in bfloat16 or wider, within the bound.
No kernel may reach another device: no remote copies, remote signals or barrier semaphores. Data moves between devices by JAX's collectives and lax.ppermute only.
A program may use at most 64 MiB of HBM per device.

```python
import jax
import jax.numpy as jnp
from jax import lax

D = 8192
FF = 32768
BLK = 128
TOKENS = 256
DB = 4
FB = 8
SLOTS = 10
N_ROW = 32
N_COL = 16


def make_slots(key, lead_first, lead_second):
    tile_count = lead_first * lead_second
    block_total = DB * FB
    key_one, key_two, key_full, key_perm = jax.random.split(key, 4)
    first_draw = jax.random.randint(key_one, (tile_count,), 0, SLOTS)
    second_draw = jax.random.randint(key_two, (tile_count,), 0, SLOTS)
    counts = 1 + (first_draw + second_draw) // 3
    full_tile = jax.random.randint(key_full, (), 0, tile_count)
    counts = jnp.where(jnp.arange(tile_count) == full_tile, SLOTS, counts)
    tile_keys = jax.random.split(key_perm, tile_count)

    def one_perm(tile_key):
        return jax.random.permutation(tile_key, block_total)
    orders = jax.vmap(one_perm)(tile_keys)[:, :SLOTS]
    slot_ids = jnp.where(jnp.arange(SLOTS)[None, :] < counts[:, None], orders, block_total)
    return slot_ids.reshape(lead_first, lead_second, SLOTS).astype(jnp.int32)


def draw_gate_slots(key, part):
    return make_slots(jax.random.fold_in(key, 11), N_COL, N_ROW)


def draw_up_slots(key, part):
    return make_slots(jax.random.fold_in(key, 23), N_COL, N_ROW)


def draw_down_slots(key, part):
    return make_slots(jax.random.fold_in(key, 37), N_ROW, N_COL)


def shard_levels(rng, shape, cuts, low, high):
    level, own = 1.0, jax.random.fold_in(rng, 6)
    for dim, parts in cuts:
        steps = jnp.exp(jax.random.uniform(jax.random.fold_in(own, dim), (parts,), jnp.float32, low / len(cuts), high / len(cuts)))
        level = level * jnp.repeat(steps, shape[dim] // parts).reshape([-1 if axis == dim else 1 for axis in range(len(shape))])
    return level


def noise(stream_key, extent, spread, most, shards=(), kind=jnp.bfloat16):
    level = shard_levels(stream_key, extent, shards, -0.22, 0.18) if shards else 1.0
    array = jax.random.normal(stream_key, extent, jnp.float32) * spread * level
    return jnp.minimum(jnp.maximum(array, -most), most).astype(kind)


def setup_inputs(seed: int = 0) -> dict:
    key_list = jax.random.split(jax.random.key(seed), 9)
    return {
        "tokens": noise(key_list[0], (TOKENS, D), 1.0, 6.0, ((0, 32), (1, 16))),
        "gate_blocks": noise(key_list[1], (N_COL, N_ROW, SLOTS, BLK, BLK), (D // 8) ** -0.5, 0.1875, ((0, 16), (1, 32))),
        "up_blocks": noise(key_list[2], (N_COL, N_ROW, SLOTS, BLK, BLK), (D // 8) ** -0.5, 0.1875, ((0, 16), (1, 32))),
        "down_blocks": noise(key_list[3], (N_ROW, N_COL, SLOTS, BLK, BLK), (FF // 8) ** -0.5, 0.09375, ((0, 32), (1, 16))),
        "gate_slots": draw_gate_slots(jax.random.fold_in(key_list[8], 71), 0),
        "up_slots": draw_up_slots(jax.random.fold_in(key_list[8], 71), 0),
        "down_slots": draw_down_slots(jax.random.fold_in(key_list[8], 71), 0),
        "out_grad": noise(key_list[7], (TOKENS, D), 1.0, 6.0, ((0, 32), (1, 16))),
    }


def slot_places(slot_ids, row_blocks, col_blocks):
    is_live = slot_ids < row_blocks * col_blocks
    row_of = jnp.minimum(slot_ids // col_blocks, row_blocks - 1)
    col_of = slot_ids % col_blocks
    return (is_live, row_of, col_of)

def wire_round(values):
    return lax.optimization_barrier(values.astype(jnp.bfloat16)).astype(jnp.float32)

def tile_forward(left_rows, blocks, slot_ids, row_blocks, col_blocks):
    tok_count = left_rows.shape[0]
    blk_width = blocks.shape[-1]
    is_live, row_of, col_of = slot_places(slot_ids, row_blocks, col_blocks)
    picked = jnp.take(left_rows.reshape(tok_count, row_blocks, blk_width), row_of, axis=1).astype(jnp.float32)
    products = jnp.einsum('tsk,skn->tsn', picked, blocks.astype(jnp.float32), precision=lax.Precision.HIGHEST)
    placing = ((col_of[:, None] == jnp.arange(col_blocks, dtype=jnp.int32)[None, :]) & is_live[:, None]).astype(jnp.float32)
    result = jnp.einsum('tsn,sc->tcn', products, placing, precision=lax.Precision.HIGHEST)
    return result.reshape(tok_count, col_blocks * blk_width)

def tile_backward(right_rows, blocks, slot_ids, row_blocks, col_blocks):
    tok_count = right_rows.shape[0]
    blk_width = blocks.shape[-1]
    is_live, row_of, col_of = slot_places(slot_ids, row_blocks, col_blocks)
    picked = jnp.take(right_rows.reshape(tok_count, col_blocks, blk_width), col_of, axis=1).astype(jnp.float32)
    products = jnp.einsum('tsn,skn->tsk', picked, blocks.astype(jnp.float32), precision=lax.Precision.HIGHEST)
    placing = ((row_of[:, None] == jnp.arange(row_blocks, dtype=jnp.int32)[None, :]) & is_live[:, None]).astype(jnp.float32)
    result = jnp.einsum('tsk,sr->trk', products, placing, precision=lax.Precision.HIGHEST)
    return result.reshape(tok_count, row_blocks * blk_width)

def tile_grad(left_rows, right_rows, slot_ids, row_blocks, col_blocks, blk_width):
    tok_count = left_rows.shape[0]
    is_live, row_of, col_of = slot_places(slot_ids, row_blocks, col_blocks)
    left_pick = jnp.take(left_rows.reshape(tok_count, row_blocks, blk_width), row_of, axis=1).astype(jnp.float32)
    right_pick = jnp.take(right_rows.reshape(tok_count, col_blocks, blk_width), col_of, axis=1).astype(jnp.float32)
    grads = jnp.einsum('tsk,tsn->skn', left_pick, right_pick, precision=lax.Precision.HIGHEST)
    return grads * is_live[:, None, None].astype(jnp.float32)

def activate(gate_val, up_val):
    return (gate_val * jax.nn.sigmoid(gate_val) * up_val).astype(jnp.bfloat16)

def gate_cotangents(hid_grad, gate_val, up_val):
    sig_val = jax.nn.sigmoid(gate_val)
    act_val = gate_val * sig_val
    slope = sig_val * (1.0 + gate_val * (1.0 - sig_val))
    return ((hid_grad * up_val * slope).astype(jnp.bfloat16), (hid_grad * act_val).astype(jnp.bfloat16))

def reference(tokens, gate_blocks, up_blocks, down_blocks, gate_slots, up_slots, down_slots, out_grad):
    tok_count = tokens.shape[0]
    blk_width = gate_blocks.shape[-1]
    dcols = D // N_COL
    fcols = FF // N_ROW
    dblocks = dcols // blk_width
    fblocks = fcols // blk_width
    tok_panels = tokens.reshape(tok_count, N_COL, dcols).transpose(1, 0, 2)
    grad_panels = out_grad.reshape(tok_count, N_COL, dcols).transpose(1, 0, 2)

    def project_row(row_idx):

        def one_tile(act_rows, gate_w, gate_s, up_w, up_s):
            return (wire_round(tile_forward(act_rows, gate_w, gate_s, dblocks, fblocks)), wire_round(tile_forward(act_rows, up_w, up_s, dblocks, fblocks)))
        gates, ups = jax.vmap(one_tile)(tok_panels, gate_blocks[:, row_idx], gate_slots[:, row_idx], up_blocks[:, row_idx], up_slots[:, row_idx])
        return (lax.optimization_barrier(jnp.sum(gates, axis=0)), lax.optimization_barrier(jnp.sum(ups, axis=0)))
    gate_rows, up_rows = lax.map(project_row, jnp.arange(N_ROW, dtype=jnp.int32))
    hidden = activate(gate_rows, up_rows)

    def output_col(col_idx):

        def one_tile(hid_rows, down_w, down_s):
            return wire_round(tile_forward(hid_rows, down_w, down_s, fblocks, dblocks))
        return lax.optimization_barrier(jnp.sum(jax.vmap(one_tile)(hidden, down_blocks[:, col_idx], down_slots[:, col_idx]), axis=0))
    out_cols = lax.map(output_col, jnp.arange(N_COL, dtype=jnp.int32))
    layer_out = out_cols.transpose(1, 0, 2).reshape(tok_count, D).astype(jnp.bfloat16)

    def hidden_row(row_idx):

        def one_tile(grad_rows, down_w, down_s):
            return wire_round(tile_backward(grad_rows, down_w, down_s, fblocks, dblocks))
        return lax.optimization_barrier(jnp.sum(jax.vmap(one_tile)(grad_panels, down_blocks[row_idx], down_slots[row_idx]), axis=0))
    hid_grad = lax.map(hidden_row, jnp.arange(N_ROW, dtype=jnp.int32))
    gate_in, up_in = gate_cotangents(hid_grad, gate_rows, up_rows)

    def down_row(row_idx):
        hid_rows = hidden[row_idx]

        def one_tile(grad_rows, down_s):
            return tile_grad(hid_rows, grad_rows, down_s, fblocks, dblocks, blk_width)
        return jax.vmap(one_tile)(grad_panels, down_slots[row_idx])
    down_grad = lax.map(down_row, jnp.arange(N_ROW, dtype=jnp.int32))

    def weight_col(col_idx):
        act_rows = tok_panels[col_idx]

        def one_tile(gate_c, up_c, gate_s, up_s):
            return (tile_grad(act_rows, gate_c, gate_s, dblocks, fblocks, blk_width), tile_grad(act_rows, up_c, up_s, dblocks, fblocks, blk_width))
        return jax.vmap(one_tile)(gate_in, up_in, gate_slots[col_idx], up_slots[col_idx])
    gate_grad, up_grad = lax.map(weight_col, jnp.arange(N_COL, dtype=jnp.int32))

    def input_col(col_idx):

        def one_tile(gate_c, up_c, gate_w, gate_s, up_w, up_s):
            return wire_round(tile_backward(gate_c, gate_w, gate_s, dblocks, fblocks) + tile_backward(up_c, up_w, up_s, dblocks, fblocks))
        terms = jax.vmap(one_tile)(gate_in, up_in, gate_blocks[col_idx], gate_slots[col_idx], up_blocks[col_idx], up_slots[col_idx])
        return lax.optimization_barrier(jnp.sum(terms, axis=0))
    in_cols = lax.map(input_col, jnp.arange(N_COL, dtype=jnp.int32))
    token_grad = in_cols.transpose(1, 0, 2).reshape(tok_count, D).astype(jnp.bfloat16)
    return (layer_out, token_grad, gate_grad, up_grad, down_grad)
```

```python
import jax
import jax.numpy as jnp
from jax import lax
from jax.experimental import pallas as pl
from jax.experimental.pallas import tpu as pltpu
from jax.sharding import PartitionSpec as P

BLK = 128
F32 = jnp.float32
BF16 = jnp.bfloat16
VMEM_BYTES = 20 * 2**20


def call(kernel, scalars, arrays, outs, scratch=(), name=None):
    in_specs = [pl.BlockSpec(memory_space=pltpu.SMEM) for _ in scalars]
    in_specs += [pl.BlockSpec(memory_space=pltpu.VMEM) for _ in arrays]
    return pl.pallas_call(
        kernel,
        out_shape=[jax.ShapeDtypeStruct(shape, dtype) for shape, dtype in outs],
        in_specs=in_specs,
        out_specs=[pl.BlockSpec(memory_space=pltpu.VMEM) for _ in outs],
        scratch_shapes=list(scratch),
        compiler_params=pltpu.CompilerParams(vmem_limit_bytes=VMEM_BYTES),
        name=name,
    )(*scalars, *arrays)


def at(index, size):
    return pl.ds(pl.multiple_of(index * size, size), size)


def dot(left, right, left_dim, right_dim):
    return lax.dot_general(
        left, right, (((left_dim,), (right_dim,)), ((), ())), preferred_element_type=F32
    )


def place_kernel(slots, gate_blk, up_blk, down_blk, gate_ref, up_ref, down_ref):
    tiles = ((gate_blk, gate_ref), (up_blk, up_ref), (down_blk, down_ref))
    for which, (blk, ref) in enumerate(tiles):
        ref[...] = jnp.zeros_like(ref)
        col_blocks = ref.shape[1] // BLK
        total = (ref.shape[0] // BLK) * col_blocks
        for slot in range(blk.shape[0]):
            number = slots[which, slot]

            @pl.when(number < total)
            def _(number=number, slot=slot, blk=blk, ref=ref, col_blocks=col_blocks):
                ref[at(number // col_blocks, BLK), at(number % col_blocks, BLK)] = blk[slot]


def partial_kernel(place, panel, gate_w, up_w, down_w, p0, p1, p2a, p2b, p3, xs):
    rows = panel.shape[0] // 4
    width = gate_w.shape[0]
    hid = gate_w.shape[1]
    half = p2a.shape[1]
    for off in range(4):
        cls = lax.rem(place[0] + off, 4)
        xs[off * rows : (off + 1) * rows, :] = panel[at(cls, rows), :]
    act, grad = xs[:, :width], xs[:, width:]
    terms = (
        dot(act, gate_w[...], 1, 0),
        dot(act, up_w[...], 1, 0),
        dot(grad, down_w[...], 1, 1),
    )
    for which, term in enumerate(terms):
        term = term.astype(BF16)
        lo = which * hid
        p0[:, lo : lo + hid] = term[:rows]
        p1[:, lo : lo + hid] = term[rows : 2 * rows]
        p3[:, lo : lo + hid] = term[3 * rows :]
        mid = term[2 * rows : 3 * rows]
        in_a = min(max(half - lo, 0), hid)
        if in_a > 0:
            p2a[:, lo : lo + in_a] = mid[:, :in_a]
        if in_a < hid:
            p2b[:, lo + in_a - half : lo + hid - half] = mid[:, in_a:]


def near_sum_kernel(place, p0, r1, r3, ra, rb, s0, s1, s2, s3):
    rows = p0.shape[0] // 4
    half = ra.shape[1]
    for off, out in enumerate((s0, s1, s2, s3)):
        part = at(lax.rem(place[1] + off, 4), rows)
        near = p0[part, :].astype(F32) + r1[part, :].astype(F32) + r3[part, :].astype(F32)
        out[:, :half] = (near[:, :half] + ra[part, :].astype(F32)).astype(out.dtype)
        out[:, half:] = (near[:, half:] + rb[part, :].astype(F32)).astype(out.dtype)


def hidden_kernel(s0, t1, t2, t3, out):
    hid = out.shape[1] // 3

    def total(which):
        cols = slice(which * hid, (which + 1) * hid)
        return (
            s0[:, cols]
            + t1[:, cols].astype(F32)
            + t2[:, cols].astype(F32)
            + t3[:, cols].astype(F32)
        )

    gate, up, cot = total(0), total(1), total(2)
    sig = jax.nn.sigmoid(gate)
    act = gate * sig
    out[:, :hid] = (act * up).astype(BF16)
    out[:, hid : 2 * hid] = (cot * up * (sig * (1.0 + gate * (1.0 - sig)))).astype(BF16)
    out[:, 2 * hid :] = (cot * act).astype(BF16)


def quad_kernel(place, own, v1, v2, v3, whole, low, high):
    rows = own.shape[0]
    half = low.shape[1]
    for off, ref in enumerate((own, v3, v2, v1)):
        part = at(lax.rem(place[1] + off, 4), rows)
        whole[part, :] = ref[...]
        low[part, :] = ref[:, :half]
        high[part, :] = ref[:, half:]


def output_kernel(place, own, w1, wa, wb, w3, gate_w, up_w, down_w, panel, out):
    rows = own.shape[0]
    half = wa.shape[1]
    hid = gate_w.shape[1]
    width = gate_w.shape[0]
    for off, ref in ((0, own), (1, w3), (3, w1)):
        panel[at(lax.rem(place[0] + off, 4), rows), :] = ref[...]
    part = at(lax.rem(place[0] + 2, 4), rows)
    panel[part, :half] = wa[...]
    panel[part, half:] = wb[...]
    out[:, :width] = dot(panel[:, :hid], down_w[...], 1, 0).astype(BF16)
    out[:, width:] = (
        dot(panel[:, hid : 2 * hid], gate_w[...], 1, 1)
        + dot(panel[:, 2 * hid :], up_w[...], 1, 1)
    ).astype(BF16)


def grad_kernel(slots, panel, hidden, gate_out, up_out, down_out, act_t, hid_t):
    width = panel.shape[1] // 2
    hid = hidden.shape[1] // 3
    for blk in range(width // BLK):
        act_t[blk] = panel[:, blk * BLK : (blk + 1) * BLK].T
    for blk in range(hid // BLK):
        hid_t[blk] = hidden[:, blk * BLK : (blk + 1) * BLK].T
    jobs = (
        (act_t, hidden, hid, hid // BLK, gate_out),
        (act_t, hidden, 2 * hid, hid // BLK, up_out),
        (hid_t, panel, width, width // BLK, down_out),
    )
    for which, (left, right, base, col_blocks, out) in enumerate(jobs):
        total = left.shape[0] * col_blocks
        for slot in range(out.shape[0]):
            number = slots[which, slot]
            live = number < total

            @pl.when(live)
            def _(number=number, slot=slot, left=left, right=right, base=base, out=out, n=col_blocks):
                cols = at(base // BLK + number % n, BLK)
                out[slot] = dot(left[number // n], right[:, cols], 1, 0)

            @pl.when(jnp.logical_not(live))
            def _(slot=slot, out=out):
                out[slot] = jnp.zeros(out.shape[1:], F32)


def sum_kernel(parts, out):
    out[...] = jnp.sum(parts[...].astype(F32), axis=0).astype(BF16)


def per_device(
    tokens, gate_blocks, up_blocks, down_blocks, gate_slots, up_slots, down_slots, out_grad
):
    n_row, n_col = lax.axis_size("row"), lax.axis_size("col")
    local, width = tokens.shape
    count = local * n_row
    share = count // n_col
    rows = share * (n_col // 4)
    hid = 8 * BLK
    wide = 3 * hid
    half = wide // 2
    z = lax.axis_index("col")
    place = jnp.stack([z % 4, z // 4]).astype(jnp.int32)
    slots = jnp.stack([gate_slots[0, 0], up_slots[0, 0], down_slots[0, 0]])

    def shift(value, dist):
        return lax.ppermute(value, "col", [(i, (i + dist) % n_col) for i in range(n_col)])

    gate_w, up_w, down_w = call(
        place_kernel,
        (slots,),
        (gate_blocks[0, 0], up_blocks[0, 0], down_blocks[0, 0]),
        (((width, hid), BF16), ((width, hid), BF16), ((hid, width), BF16)),
        name="place",
    )
    both = jnp.concatenate([tokens, out_grad], axis=1)
    spread = jnp.broadcast_to(both[None], (n_row, local, 2 * width))
    panel = lax.all_to_all(spread, "row", 0, 0, tiled=True).reshape(count, 2 * width)

    p0, p1, p2a, p2b, p3 = call(
        partial_kernel,
        (place,),
        (panel, gate_w, up_w, down_w),
        (
            ((rows, wide), BF16),
            ((rows, wide), BF16),
            ((rows, half), BF16),
            ((rows, half), BF16),
            ((rows, wide), BF16),
        ),
        (pltpu.VMEM((count, 2 * width), BF16),),
        name="partials",
    )
    r1, r3, ra, rb = shift(p1, 1), shift(p3, -1), shift(p2a, -2), shift(p2b, 2)
    s0, s1, s2, s3 = call(
        near_sum_kernel,
        (place,),
        (p0, r1, r3, ra, rb),
        (((share, wide), F32),) + (((share, wide), BF16),) * 3,
        name="near_sum",
    )
    t1, t3, t2 = shift(s1, 4), shift(s3, -4), shift(s2, 8)
    (own,) = call(hidden_kernel, (), (s0, t1, t2, t3), (((share, wide), BF16),), name="hidden")

    v1, v3, v2 = shift(own, 4), shift(own, -4), shift(own, 8)
    whole, low, high = call(
        quad_kernel,
        (place,),
        (own, v1, v2, v3),
        (((rows, wide), BF16), ((rows, half), BF16), ((rows, half), BF16)),
        name="quad",
    )
    w1, w3, wa, wb = shift(whole, 1), shift(whole, -1), shift(low, 2), shift(high, -2)
    hidden, out_terms = call(
        output_kernel,
        (place,),
        (whole, w1, wa, wb, w3, gate_w, up_w, down_w),
        (((count, wide), BF16), ((count, 2 * width), BF16)),
        name="outputs",
    )
    parts = lax.all_to_all(
        out_terms.reshape(n_row, local, 2 * width), "row", 0, 0, tiled=True
    )
    gate_grad, up_grad, down_grad = call(
        grad_kernel,
        (slots,),
        (panel, hidden),
        tuple((ref.shape[2:], F32) for ref in (gate_blocks, up_blocks, down_blocks)),
        (
            pltpu.VMEM((width // BLK, BLK, count), BF16),
            pltpu.VMEM((hid // BLK, BLK, count), BF16),
        ),
        name="grads",
    )
    (summed,) = call(sum_kernel, (), (parts,), (((local, 2 * width), BF16),), name="row_sum")
    return (
        summed[:, :width],
        summed[:, width:],
        gate_grad[None, None],
        up_grad[None, None],
        down_grad[None, None],
    )


def solution(mesh):
    in_specs = (
        P("row", "col"),
        P("col", "row", None, None, None),
        P("col", "row", None, None, None),
        P("row", "col", None, None, None),
        P("col", "row", None),
        P("col", "row", None),
        P("row", "col", None),
        P("row", "col"),
    )
    out_specs = (
        P("row", "col"),
        P("row", "col"),
        P("col", "row", None, None, None),
        P("col", "row", None, None, None),
        P("row", "col", None, None, None),
    )
    return jax.shard_map(
        per_device, mesh=mesh, in_specs=in_specs, out_specs=out_specs, check_vma=False
    )
```

```python
import jax
import jax.numpy as jnp
from jax import lax
from jax.experimental import pallas as pl
from jax.experimental.pallas import tpu as pltpu
from jax.sharding import PartitionSpec as P

BLK = 128
F32 = jnp.float32
BF16 = jnp.bfloat16
FLOOR = 2.0**-100
VMEM_BYTES = 20 * 2**20


def call(kernel, scalars, arrays, outs, scratch=(), name=None):
    in_specs = [pl.BlockSpec(memory_space=pltpu.SMEM) for _ in scalars]
    in_specs += [pl.BlockSpec(memory_space=pltpu.VMEM) for _ in arrays]
    return pl.pallas_call(
        kernel,
        out_shape=[jax.ShapeDtypeStruct(shape, dtype) for shape, dtype in outs],
        in_specs=in_specs,
        out_specs=[pl.BlockSpec(memory_space=pltpu.VMEM) for _ in outs],
        scratch_shapes=list(scratch),
        compiler_params=pltpu.CompilerParams(vmem_limit_bytes=VMEM_BYTES),
        name=name,
    )(*scalars, *arrays)


def at(index, size):
    return pl.ds(pl.multiple_of(index * size, size), size)


def dot(left, right, left_dim, right_dim):
    return lax.dot_general(
        left, right, (((left_dim,), (right_dim,)), ((), ())), preferred_element_type=F32
    )


def place_kernel(slots, gate_blk, up_blk, down_blk, gate_ref, up_ref, down_ref):
    tiles = ((gate_blk, gate_ref), (up_blk, up_ref), (down_blk, down_ref))
    for which, (blk, ref) in enumerate(tiles):
        ref[...] = jnp.zeros_like(ref)
        col_blocks = ref.shape[1] // BLK
        total = (ref.shape[0] // BLK) * col_blocks
        for slot in range(blk.shape[0]):
            number = slots[which, slot]

            @pl.when(number < total)
            def _(number=number, slot=slot, blk=blk, ref=ref, col_blocks=col_blocks):
                ref[at(number // col_blocks, BLK), at(number % col_blocks, BLK)] = blk[slot]


def partial_kernel(place, panel, gate_w, up_w, down_w, p0, p1, p2a, p2b, p3, xs):
    rows = panel.shape[0] // 4
    width = gate_w.shape[0]
    hid = gate_w.shape[1]
    half = p2a.shape[1]
    for off in range(4):
        cls = lax.rem(place[0] + off, 4)
        xs[off * rows : (off + 1) * rows, :] = panel[at(cls, rows), :]
    act, grad = xs[:, :width], xs[:, width:]
    terms = (
        dot(act, gate_w[...], 1, 0),
        dot(act, up_w[...], 1, 0),
        dot(grad, down_w[...], 1, 1),
    )
    for which, term in enumerate(terms):
        term = term.astype(BF16)
        lo = which * hid
        p0[:, lo : lo + hid] = term[:rows]
        p1[:, lo : lo + hid] = term[rows : 2 * rows]
        p3[:, lo : lo + hid] = term[3 * rows :]
        mid = term[2 * rows : 3 * rows]
        in_a = min(max(half - lo, 0), hid)
        if in_a > 0:
            p2a[:, lo : lo + in_a] = mid[:, :in_a]
        if in_a < hid:
            p2b[:, lo + in_a - half : lo + hid - half] = mid[:, in_a:]


def near_sum_kernel(place, p0, r1, r3, ra, rb, s0, s1, s2, s3):
    rows = p0.shape[0] // 4
    half = ra.shape[1]
    for off, out in enumerate((s0, s1, s2, s3)):
        part = at(lax.rem(place[1] + off, 4), rows)
        near = p0[part, :].astype(F32) + r1[part, :].astype(F32) + r3[part, :].astype(F32)
        out[:, :half] = (near[:, :half] + ra[part, :].astype(F32)).astype(out.dtype)
        out[:, half:] = (near[:, half:] + rb[part, :].astype(F32)).astype(out.dtype)


def hidden_kernel(s0, t1, t2, t3, out):
    hid = s0.shape[1] // 3

    def total(which):
        cols = slice(which * hid, (which + 1) * hid)
        return (
            s0[:, cols]
            + t1[:, cols].astype(F32)
            + t2[:, cols].astype(F32)
            + t3[:, cols].astype(F32)
        )

    gate, up, cot = total(0), total(1), total(2)
    sig = jax.nn.sigmoid(gate)
    act = gate * sig
    results = (act * up, cot * up * (sig * (1.0 + gate * (1.0 - sig))), cot * act)
    rows = out.shape[0]
    lane = lax.broadcasted_iota(jnp.int32, (rows, BLK), 1)
    powers = jnp.zeros((rows, BLK), F32)
    for which, value in enumerate(results):
        value = value.astype(BF16).astype(F32)
        most = jnp.max(jnp.abs(value), axis=1, keepdims=True)
        power = jnp.floor(jnp.log2(jnp.maximum(most, FLOOR)))
        out[:, which * hid : (which + 1) * hid] = value * jnp.exp2(13.0 - power)
        powers = jnp.where(lane == which, power, powers)
    out[:, 3 * hid :] = powers


def output_kernel(gathered, gate_w, up_w, down_w, panel, out):
    hid = gate_w.shape[1]
    width = gate_w.shape[0]
    share = gathered.shape[0] // 16
    for dev in range(16):
        src = slice(dev * share, (dev + 1) * share)
        dst = (4 * (dev % 4) + dev // 4) * share
        powers = gathered[src, 3 * hid :].astype(F32)
        for which in range(3):
            cols = slice(which * hid, (which + 1) * hid)
            scale = jnp.exp2(powers[:, which : which + 1] - 13.0)
            panel[dst : dst + share, cols] = (gathered[src, cols].astype(F32) * scale).astype(BF16)
    out[:, :width] = dot(panel[:, :hid], down_w[...], 1, 0).astype(BF16)
    out[:, width:] = (
        dot(panel[:, hid : 2 * hid], gate_w[...], 1, 1)
        + dot(panel[:, 2 * hid :], up_w[...], 1, 1)
    ).astype(BF16)


def grad_kernel(slots, panel, hidden, gate_out, up_out, down_out, act_t, hid_t):
    width = panel.shape[1] // 2
    hid = hidden.shape[1] // 3
    for blk in range(width // BLK):
        act_t[blk] = panel[:, blk * BLK : (blk + 1) * BLK].T
    for blk in range(hid // BLK):
        hid_t[blk] = hidden[:, blk * BLK : (blk + 1) * BLK].T
    jobs = (
        (act_t, hidden, hid, hid // BLK, gate_out),
        (act_t, hidden, 2 * hid, hid // BLK, up_out),
        (hid_t, panel, width, width // BLK, down_out),
    )
    for which, (left, right, base, col_blocks, out) in enumerate(jobs):
        total = left.shape[0] * col_blocks
        for slot in range(out.shape[0]):
            number = slots[which, slot]
            live = number < total

            @pl.when(live)
            def _(number=number, slot=slot, left=left, right=right, base=base, out=out, n=col_blocks):
                cols = at(base // BLK + number % n, BLK)
                out[slot] = dot(left[number // n], right[:, cols], 1, 0)

            @pl.when(jnp.logical_not(live))
            def _(slot=slot, out=out):
                out[slot] = jnp.zeros(out.shape[1:], F32)


def sum_kernel(parts, out):
    out[...] = jnp.sum(parts[...].astype(F32), axis=0).astype(BF16)


def per_device(
    tokens, gate_blocks, up_blocks, down_blocks, gate_slots, up_slots, down_slots, out_grad
):
    n_row, n_col = lax.axis_size("row"), lax.axis_size("col")
    local, width = tokens.shape
    count = local * n_row
    share = count // n_col
    rows = share * (n_col // 4)
    hid = 8 * BLK
    wide = 3 * hid
    half = wide // 2
    z = lax.axis_index("col")
    place = jnp.stack([z % 4, z // 4]).astype(jnp.int32)
    slots = jnp.stack([gate_slots[0, 0], up_slots[0, 0], down_slots[0, 0]])

    def shift(value, dist):
        return lax.ppermute(value, "col", [(i, (i + dist) % n_col) for i in range(n_col)])

    gate_w, up_w, down_w = call(
        place_kernel,
        (slots,),
        (gate_blocks[0, 0], up_blocks[0, 0], down_blocks[0, 0]),
        (((width, hid), BF16), ((width, hid), BF16), ((hid, width), BF16)),
        name="place",
    )
    both = jnp.concatenate([tokens, out_grad], axis=1)
    spread = jnp.broadcast_to(both[None], (n_row, local, 2 * width))
    panel = lax.all_to_all(spread, "row", 0, 0, tiled=True).reshape(count, 2 * width)

    p0, p1, p2a, p2b, p3 = call(
        partial_kernel,
        (place,),
        (panel, gate_w, up_w, down_w),
        (
            ((rows, wide), BF16),
            ((rows, wide), BF16),
            ((rows, half), BF16),
            ((rows, half), BF16),
            ((rows, wide), BF16),
        ),
        (pltpu.VMEM((count, 2 * width), BF16),),
        name="partials",
    )
    r1, r3, ra, rb = shift(p1, 1), shift(p3, -1), shift(p2a, -2), shift(p2b, 2)
    s0, s1, s2, s3 = call(
        near_sum_kernel,
        (place,),
        (p0, r1, r3, ra, rb),
        (((share, wide), F32),) + (((share, wide), BF16),) * 3,
        name="near_sum",
    )
    t1, t3, t2 = shift(s1, 4), shift(s3, -4), shift(s2, 8)
    (own,) = call(
        hidden_kernel, (), (s0, t1, t2, t3), (((share, wide + BLK), F32),), name="hidden"
    )
    gathered = lax.all_gather(own.astype(jnp.float16), "col", axis=0, tiled=True).astype(BF16)
    hidden, out_terms = call(
        output_kernel,
        (),
        (gathered, gate_w, up_w, down_w),
        (((count, wide), BF16), ((count, 2 * width), BF16)),
        name="outputs",
    )
    parts = lax.all_to_all(
        out_terms.reshape(n_row, local, 2 * width), "row", 0, 0, tiled=True
    )
    gate_grad, up_grad, down_grad = call(
        grad_kernel,
        (slots,),
        (panel, hidden),
        tuple((ref.shape[2:], F32) for ref in (gate_blocks, up_blocks, down_blocks)),
        (
            pltpu.VMEM((width // BLK, BLK, count), BF16),
            pltpu.VMEM((hid // BLK, BLK, count), BF16),
        ),
        name="grads",
    )
    (summed,) = call(sum_kernel, (), (parts,), (((local, 2 * width), BF16),), name="row_sum")
    return (
        summed[:, :width],
        summed[:, width:],
        gate_grad[None, None],
        up_grad[None, None],
        down_grad[None, None],
    )


def solution(mesh):
    in_specs = (
        P("row", "col"),
        P("col", "row", None, None, None),
        P("col", "row", None, None, None),
        P("row", "col", None, None, None),
        P("col", "row", None),
        P("col", "row", None),
        P("row", "col", None),
        P("row", "col"),
    )
    out_specs = (
        P("row", "col"),
        P("row", "col"),
        P("col", "row", None, None, None),
        P("col", "row", None, None, None),
        P("row", "col", None, None, None),
    )
    return jax.shard_map(
        per_device, mesh=mesh, in_specs=in_specs, out_specs=out_specs, check_vma=False
    )
```

```python
import jax
import jax.numpy as jnp
import numpy as np
from jax import lax
from jax.experimental import pallas as pl
from jax.experimental.pallas import tpu as pltpu
from jax.sharding import PartitionSpec as P

BLK = 128
F32 = jnp.float32
BF16 = jnp.bfloat16
FLOOR = 2.0**-100
VMEM_BYTES = 20 * 2**20


def call(kernel, scalars, arrays, outs, scratch=(), name=None, far=(), far_outs=()):
    arrays = [
        pltpu.with_memory_space_constraint(array, pltpu.HBM) if i in far else array
        for i, array in enumerate(arrays)
    ]
    in_specs = [pl.BlockSpec(memory_space=pltpu.SMEM) for _ in scalars]
    in_specs += [
        pl.BlockSpec(memory_space=pltpu.HBM if i in far else pltpu.VMEM)
        for i in range(len(arrays))
    ]
    return pl.pallas_call(
        kernel,
        out_shape=[
            pltpu.HBM(*out) if i in far_outs else jax.ShapeDtypeStruct(*out)
            for i, out in enumerate(outs)
        ],
        in_specs=in_specs,
        out_specs=[
            pl.BlockSpec(memory_space=pltpu.HBM if i in far_outs else pltpu.VMEM)
            for i in range(len(outs))
        ],
        scratch_shapes=list(scratch),
        compiler_params=pltpu.CompilerParams(vmem_limit_bytes=VMEM_BYTES),
        name=name,
    )(*scalars, *arrays)


def at(index, size):
    return pl.ds(pl.multiple_of(index * size, size), size)


def dot(left, right, left_dim, right_dim):
    return lax.dot_general(
        left, right, (((left_dim,), (right_dim,)), ((), ())), preferred_element_type=F32
    )


def spread_kernel(tokens, grads, out):
    width = tokens.shape[1]
    out[:, :, :width] = jnp.broadcast_to(tokens[...][None], (out.shape[0],) + tokens.shape)
    out[:, :, width:] = jnp.broadcast_to(grads[...][None], (out.shape[0],) + grads.shape)


def place_kernel(
    slots, gate_blk, up_blk, down_blk, gate_ref, up_out, down_out, up_ref, down_ref, sems
):
    tiles = ((down_blk, down_ref, 2), (up_blk, up_ref, 1), (gate_blk, gate_ref, 0))
    copies = {
        1: pltpu.make_async_copy(up_ref, up_out, sems.at[0]),
        2: pltpu.make_async_copy(down_ref, down_out, sems.at[1]),
    }
    for blk, ref, which in tiles:
        ref[...] = jnp.zeros_like(ref)
        col_blocks = ref.shape[1] // BLK
        total = (ref.shape[0] // BLK) * col_blocks
        for slot in range(blk.shape[0]):
            number = slots[which, slot]

            @pl.when(number < total)
            def _(number=number, slot=slot, blk=blk, ref=ref, col_blocks=col_blocks):
                ref[at(number // col_blocks, BLK), at(number % col_blocks, BLK)] = blk[slot]

        if which > 0:
            copies[which].start()
    copies[1].wait()
    copies[2].wait()


def row_moves(share, n_col):
    keep = share - 1
    rows = np.zeros((n_col * keep, n_col * share), np.float32)
    last = np.zeros((n_col, n_col * share), np.float32)
    spot = np.zeros((n_col * keep, 8 * n_col), np.float32)
    for dev in range(n_col):
        last[dev, dev * share + keep] = 1.0
        for row in range(keep):
            rows[dev * keep + row, dev * share + row] = 1.0
        for blk in range(8):
            spot[dev * keep + blk, blk * n_col + dev] = 1.0
    return tuple(jnp.asarray(m, BF16) for m in (rows, last, spot))


def partial_kernel(panel, gate_w, rows, last, spot, up_far, down_far, out, up_w, down_w, sems):
    copies = {
        1: pltpu.make_async_copy(up_far, up_w, sems.at[0]),
        2: pltpu.make_async_copy(down_far, down_w, sems.at[1]),
    }
    copies[1].start()
    copies[2].start()
    width, hid = gate_w.shape
    main = dot(rows[...], panel[...], 1, 0).astype(BF16)
    ends = dot(last[...], panel[...], 1, 0).astype(BF16)
    jobs = ((0, gate_w, 0), (0, up_w, 0), (width, down_w, 1))
    for which, (lo, weight, dim) in enumerate(jobs):
        if which > 0:
            copies[which].wait()
        base = which * (hid + BLK)
        tile = weight[...]
        out[:, base : base + hid] = dot(main[:, lo : lo + width], tile, 1, dim).astype(BF16)
        end = dot(ends[:, lo : lo + width], tile, 1, dim).astype(BF16)
        pieces = [end[:, blk * BLK : (blk + 1) * BLK] for blk in range(hid // BLK)]
        moved = dot(spot[...], jnp.concatenate(pieces, axis=0), 1, 0)
        out[:, base + hid : base + hid + BLK] = moved.astype(BF16)


def hidden_kernel(sums, out, full):
    keep = sums.shape[0]
    step = sums.shape[1] // 3
    hid = step - BLK
    gate, up, cot = (sums[:, i * step : (i + 1) * step].astype(F32) for i in range(3))
    sig = jax.nn.sigmoid(gate)
    act = gate * sig
    results = (act * up, cot * up * (sig * (1.0 + gate * (1.0 - sig))), cot * act)
    lane = lax.broadcasted_iota(jnp.int32, (keep + 1, BLK), 1)
    powers = jnp.zeros((keep + 1, BLK), F32)
    for which, value in enumerate(results):
        value = value.astype(BF16).astype(F32)
        full[0:keep, :] = value[:, :hid]
        for blk in range(hid // BLK):
            full[keep : keep + 1, blk * BLK : (blk + 1) * BLK] = value[blk : blk + 1, hid:]
        value = full[...]
        most = jnp.max(jnp.abs(value), axis=1, keepdims=True)
        power = jnp.floor(jnp.log2(jnp.maximum(most, FLOOR)))
        out[:, which * hid : (which + 1) * hid] = value * jnp.exp2(13.0 - power)
        powers = jnp.where(lane == which, power, powers)
    out[:, 3 * hid :] = powers


def output_kernel(
    gathered, gate_w, up_far, down_far, panel_out, out, panel, up_w, down_w, sems
):
    load_up = pltpu.make_async_copy(up_far, up_w, sems.at[0])
    load = pltpu.make_async_copy(down_far, down_w, sems.at[1])
    store = pltpu.make_async_copy(panel, panel_out, sems.at[2])
    load_up.start()
    load.start()
    width, hid = gate_w.shape
    powers = gathered[:, 3 * hid :].astype(F32)
    for which in range(3):
        cols = slice(which * hid, (which + 1) * hid)
        scale = jnp.exp2(powers[:, which : which + 1] - 13.0)
        panel[:, cols] = (gathered[:, cols].astype(F32) * scale).astype(BF16)
    store.start()
    load_up.wait()
    out[:, width:] = (
        dot(panel[:, hid : 2 * hid], gate_w[...], 1, 1)
        + dot(panel[:, 2 * hid :], up_w[...], 1, 1)
    ).astype(BF16)
    load.wait()
    out[:, :width] = dot(panel[:, :hid], down_w[...], 1, 0).astype(BF16)
    store.wait()


def grad_kernel(slots, panel, hidden, gate_out, up_out, down_out, act_t, hid_t):
    width = panel.shape[1] // 2
    hid = hidden.shape[1] // 3
    for blk in range(width // BLK):
        act_t[blk] = panel[:, blk * BLK : (blk + 1) * BLK].T
    for blk in range(hid // BLK):
        hid_t[blk] = hidden[:, blk * BLK : (blk + 1) * BLK].T
    jobs = (
        (act_t, hidden, hid, hid // BLK, gate_out),
        (act_t, hidden, 2 * hid, hid // BLK, up_out),
        (hid_t, panel, width, width // BLK, down_out),
    )
    for which, (left, right, base, col_blocks, out) in enumerate(jobs):
        total = left.shape[0] * col_blocks
        for slot in range(out.shape[0]):
            number = slots[which, slot]
            live = number < total

            @pl.when(live)
            def _(number=number, slot=slot, left=left, right=right, base=base, out=out, n=col_blocks):
                cols = at(base // BLK + number % n, BLK)
                out[slot] = dot(left[number // n], right[:, cols], 1, 0)

            @pl.when(jnp.logical_not(live))
            def _(slot=slot, out=out):
                out[slot] = jnp.zeros(out.shape[1:], F32)


def sum_kernel(parts, first, second):
    total = jnp.sum(parts[...].astype(F32), axis=0).astype(BF16)
    first[...] = total[:, : first.shape[1]]
    second[...] = total[:, first.shape[1] :]


def per_device(
    tokens, gate_blocks, up_blocks, down_blocks, gate_slots, up_slots, down_slots, out_grad
):
    n_row, n_col = lax.axis_size("row"), lax.axis_size("col")
    local, width = tokens.shape
    count = local * n_row
    share = count // n_col
    hid = 8 * BLK
    wide = 3 * hid
    slots = jnp.stack([gate_slots[0, 0], up_slots[0, 0], down_slots[0, 0]])

    gate_w, up_w, down_w = call(
        place_kernel,
        (slots,),
        (gate_blocks[0, 0], up_blocks[0, 0], down_blocks[0, 0]),
        (((width, hid), BF16), ((width, hid), BF16), ((hid, width), BF16)),
        (
            pltpu.VMEM((width, hid), BF16),
            pltpu.VMEM((hid, width), BF16),
            pltpu.SemaphoreType.DMA((2,)),
        ),
        name="place",
        far_outs=(1, 2),
    )
    (spread,) = call(
        spread_kernel, (), (tokens, out_grad), (((n_row, local, 2 * width), BF16),), name="spread"
    )
    panel = lax.all_to_all(spread, "row", 0, 0, tiled=True).reshape(count, 2 * width)

    (terms,) = call(
        partial_kernel,
        (),
        (panel, gate_w) + row_moves(share, n_col) + (up_w, down_w),
        (((n_col * (share - 1), wide + 3 * BLK), BF16),),
        (
            pltpu.VMEM((width, hid), BF16),
            pltpu.VMEM((hid, width), BF16),
            pltpu.SemaphoreType.DMA((2,)),
        ),
        name="partials",
        far=(5, 6),
    )
    sums = lax.psum_scatter(terms, "col", scatter_dimension=0, tiled=True)
    (own,) = call(
        hidden_kernel,
        (),
        (sums,),
        (((share, wide + BLK), F32),),
        (pltpu.VMEM((share, hid), F32),),
        name="hidden",
    )
    gathered = lax.all_gather(own.astype(jnp.float16), "col", axis=0, tiled=True).astype(BF16)
    hidden, out_terms = call(
        output_kernel,
        (),
        (gathered, gate_w, up_w, down_w),
        (((count, wide), BF16), ((count, 2 * width), BF16)),
        (
            pltpu.VMEM((count, wide), BF16),
            pltpu.VMEM((width, hid), BF16),
            pltpu.VMEM((hid, width), BF16),
            pltpu.SemaphoreType.DMA((3,)),
        ),
        name="outputs",
        far=(2, 3),
        far_outs=(0,),
    )
    parts = lax.all_to_all(
        out_terms.reshape(n_row, local, 2 * width), "row", 0, 0, tiled=True
    )
    gate_grad, up_grad, down_grad = call(
        grad_kernel,
        (slots,),
        (panel, hidden),
        tuple((ref.shape[2:], F32) for ref in (gate_blocks, up_blocks, down_blocks)),
        (
            pltpu.VMEM((width // BLK, BLK, count), BF16),
            pltpu.VMEM((hid // BLK, BLK, count), BF16),
        ),
        name="grads",
    )
    layer_out, token_grad = call(
        sum_kernel, (), (parts,), (((local, width), BF16),) * 2, name="row_sum"
    )
    return (
        layer_out,
        token_grad,
        gate_grad[None, None],
        up_grad[None, None],
        down_grad[None, None],
    )


def solution(mesh):
    in_specs = (
        P("row", "col"),
        P("col", "row", None, None, None),
        P("col", "row", None, None, None),
        P("row", "col", None, None, None),
        P("col", "row", None),
        P("col", "row", None),
        P("row", "col", None),
        P("row", "col"),
    )
    out_specs = (
        P("row", "col"),
        P("row", "col"),
        P("col", "row", None, None, None),
        P("col", "row", None, None, None),
        P("row", "col", None, None, None),
    )
    return jax.shard_map(
        per_device, mesh=mesh, in_specs=in_specs, out_specs=out_specs, check_vma=False
    )
```

```python
import jax
import jax.numpy as jnp
from jax import lax
from jax.experimental import pallas as pl
from jax.experimental.pallas import tpu as pltpu
from jax.sharding import PartitionSpec as P

BLK = 128
F32 = jnp.float32
BF16 = jnp.bfloat16
GROUP = 64
VMEM_BYTES = 20 * 2**20


def call(kernel, scalars, arrays, outs, scratch=(), name=None, far=(), far_outs=()):
    arrays = [
        pltpu.with_memory_space_constraint(array, pltpu.HBM) if i in far else array
        for i, array in enumerate(arrays)
    ]
    in_specs = [pl.BlockSpec(memory_space=pltpu.SMEM) for _ in scalars]
    in_specs += [
        pl.BlockSpec(memory_space=pltpu.HBM if i in far else pltpu.VMEM)
        for i in range(len(arrays))
    ]
    return pl.pallas_call(
        kernel,
        out_shape=[
            pltpu.HBM(*out) if i in far_outs else jax.ShapeDtypeStruct(*out)
            for i, out in enumerate(outs)
        ],
        in_specs=in_specs,
        out_specs=[
            pl.BlockSpec(memory_space=pltpu.HBM if i in far_outs else pltpu.VMEM)
            for i in range(len(outs))
        ],
        scratch_shapes=list(scratch),
        compiler_params=pltpu.CompilerParams(vmem_limit_bytes=VMEM_BYTES),
        name=name,
    )(*scalars, *arrays)


def at(index, size):
    return pl.ds(pl.multiple_of(index * size, size), size)


def dot(left, right, left_dim, right_dim):
    return lax.dot_general(
        left, right, (((left_dim,), (right_dim,)), ((), ())), preferred_element_type=F32
    )


def spread_kernel(tokens, grads, out):
    width = tokens.shape[1]
    out[:, :, :width] = jnp.broadcast_to(tokens[...][None], (out.shape[0],) + tokens.shape)
    out[:, :, width:] = jnp.broadcast_to(grads[...][None], (out.shape[0],) + grads.shape)


def place_kernel(
    slots, gate_blk, up_blk, down_blk, gate_ref, up_out, down_out, up_ref, down_ref, sems
):
    tiles = ((down_blk, down_ref, 2), (up_blk, up_ref, 1), (gate_blk, gate_ref, 0))
    copies = {
        1: pltpu.make_async_copy(up_ref, up_out, sems.at[0]),
        2: pltpu.make_async_copy(down_ref, down_out, sems.at[1]),
    }
    for blk, ref, which in tiles:
        ref[...] = jnp.zeros_like(ref)
        col_blocks = ref.shape[1] // BLK
        total = (ref.shape[0] // BLK) * col_blocks
        for slot in range(blk.shape[0]):
            number = slots[which, slot]

            @pl.when(number < total)
            def _(number=number, slot=slot, blk=blk, ref=ref, col_blocks=col_blocks):
                ref[at(number // col_blocks, BLK), at(number % col_blocks, BLK)] = blk[slot]

        if which > 0:
            copies[which].start()
    copies[1].wait()
    copies[2].wait()


def partial_kernel(panel, gate_w, up_far, down_far, *refs):
    outs, (up_w, down_w, sems) = refs[:-3], refs[-3:]
    copies = {
        1: pltpu.make_async_copy(up_far, up_w, sems.at[0]),
        2: pltpu.make_async_copy(down_far, down_w, sems.at[1]),
    }
    copies[1].start()
    copies[2].start()
    width, hid = gate_w.shape
    blocks = hid // BLK
    jobs = ((0, gate_w, 0), (0, up_w, 0), (width, down_w, 1))
    each = len(outs) // 3
    for which, (lo, weight, dim) in enumerate(jobs):
        if which > 0:
            copies[which].wait()
        term = dot(panel[:, lo : lo + width], weight[...], 1, dim).astype(BF16)
        for i in range(each):
            row, col = (i // blocks) * GROUP, (i % blocks) * BLK
            outs[which * each + i][...] = term[row : row + GROUP, col : col + BLK]


def output_kernel(gate_w, up_far, down_far, *refs):
    sums, (panel_out, out, panel, up_w, down_w, sems) = refs[:-6], refs[-6:]
    load_up = pltpu.make_async_copy(up_far, up_w, sems.at[0])
    load = pltpu.make_async_copy(down_far, down_w, sems.at[1])
    store = pltpu.make_async_copy(panel, panel_out, sems.at[2])
    load_up.start()
    load.start()
    width, hid = gate_w.shape
    blocks = hid // BLK
    each = len(sums) // 3
    for i in range(each):
        gate, up, cot = (sums[k * each + i][...].astype(F32) for k in range(3))
        sig = jax.nn.sigmoid(gate)
        act = gate * sig
        rows = slice((i // blocks) * GROUP, (i // blocks + 1) * GROUP)
        col = (i % blocks) * BLK
        panel[rows, col : col + BLK] = (act * up).astype(BF16)
        panel[rows, hid + col : hid + col + BLK] = (
            cot * up * (sig * (1.0 + gate * (1.0 - sig)))
        ).astype(BF16)
        panel[rows, 2 * hid + col : 2 * hid + col + BLK] = (cot * act).astype(BF16)
    store.start()
    load_up.wait()
    out[:, width:] = (
        dot(panel[:, hid : 2 * hid], gate_w[...], 1, 1)
        + dot(panel[:, 2 * hid :], up_w[...], 1, 1)
    ).astype(BF16)
    load.wait()
    out[:, :width] = dot(panel[:, :hid], down_w[...], 1, 0).astype(BF16)
    store.wait()


def grad_kernel(slots, panel, hidden, gate_out, up_out, down_out, act_t, hid_t):
    width = panel.shape[1] // 2
    hid = hidden.shape[1] // 3
    for blk in range(width // BLK):
        act_t[blk] = panel[:, blk * BLK : (blk + 1) * BLK].T
    for blk in range(hid // BLK):
        hid_t[blk] = hidden[:, blk * BLK : (blk + 1) * BLK].T
    jobs = (
        (act_t, hidden, hid, hid // BLK, gate_out),
        (act_t, hidden, 2 * hid, hid // BLK, up_out),
        (hid_t, panel, width, width // BLK, down_out),
    )
    for which, (left, right, base, col_blocks, out) in enumerate(jobs):
        total = left.shape[0] * col_blocks
        for slot in range(out.shape[0]):
            number = slots[which, slot]
            live = number < total

            @pl.when(live)
            def _(number=number, slot=slot, left=left, right=right, base=base, out=out, n=col_blocks):
                cols = at(base // BLK + number % n, BLK)
                out[slot] = dot(left[number // n], right[:, cols], 1, 0)

            @pl.when(jnp.logical_not(live))
            def _(slot=slot, out=out):
                out[slot] = jnp.zeros(out.shape[1:], F32)


def sum_kernel(parts, first, second):
    total = jnp.sum(parts[...].astype(F32), axis=0).astype(BF16)
    first[...] = total[:, : first.shape[1]]
    second[...] = total[:, first.shape[1] :]


def per_device(
    tokens, gate_blocks, up_blocks, down_blocks, gate_slots, up_slots, down_slots, out_grad
):
    n_row = lax.axis_size("row")
    local, width = tokens.shape
    count = local * n_row
    hid = 8 * BLK
    wide = 3 * hid
    slots = jnp.stack([gate_slots[0, 0], up_slots[0, 0], down_slots[0, 0]])

    gate_w, up_w, down_w = call(
        place_kernel,
        (slots,),
        (gate_blocks[0, 0], up_blocks[0, 0], down_blocks[0, 0]),
        (((width, hid), BF16), ((width, hid), BF16), ((hid, width), BF16)),
        (
            pltpu.VMEM((width, hid), BF16),
            pltpu.VMEM((hid, width), BF16),
            pltpu.SemaphoreType.DMA((2,)),
        ),
        name="place",
        far_outs=(1, 2),
    )
    (spread,) = call(
        spread_kernel, (), (tokens, out_grad), (((n_row, local, 2 * width), BF16),), name="spread"
    )
    panel = lax.all_to_all(spread, "row", 0, 0, tiled=True).reshape(count, 2 * width)

    terms = call(
        partial_kernel,
        (),
        (panel, gate_w, up_w, down_w),
        (((GROUP, BLK), BF16),) * (3 * (count // GROUP) * (hid // BLK)),
        (
            pltpu.VMEM((width, hid), BF16),
            pltpu.VMEM((hid, width), BF16),
            pltpu.SemaphoreType.DMA((2,)),
        ),
        name="partials",
        far=(2, 3),
    )
    sums = lax.psum(tuple(terms), "col")
    hidden, out_terms = call(
        output_kernel,
        (),
        (gate_w, up_w, down_w) + tuple(sums),
        (((count, wide), BF16), ((count, 2 * width), BF16)),
        (
            pltpu.VMEM((count, wide), BF16),
            pltpu.VMEM((width, hid), BF16),
            pltpu.VMEM((hid, width), BF16),
            pltpu.SemaphoreType.DMA((3,)),
        ),
        name="outputs",
        far=(1, 2),
        far_outs=(0,),
    )
    parts = lax.all_to_all(
        out_terms.reshape(n_row, local, 2 * width), "row", 0, 0, tiled=True
    )
    gate_grad, up_grad, down_grad = call(
        grad_kernel,
        (slots,),
        (panel, hidden),
        tuple((ref.shape[2:], F32) for ref in (gate_blocks, up_blocks, down_blocks)),
        (
            pltpu.VMEM((width // BLK, BLK, count), BF16),
            pltpu.VMEM((hid // BLK, BLK, count), BF16),
        ),
        name="grads",
    )
    layer_out, token_grad = call(
        sum_kernel, (), (parts,), (((local, width), BF16),) * 2, name="row_sum"
    )
    return (
        layer_out,
        token_grad,
        gate_grad[None, None],
        up_grad[None, None],
        down_grad[None, None],
    )


def solution(mesh):
    in_specs = (
        P("row", "col"),
        P("col", "row", None, None, None),
        P("col", "row", None, None, None),
        P("row", "col", None, None, None),
        P("col", "row", None),
        P("col", "row", None),
        P("row", "col", None),
        P("row", "col"),
    )
    out_specs = (
        P("row", "col"),
        P("row", "col"),
        P("col", "row", None, None, None),
        P("col", "row", None, None, None),
        P("row", "col", None, None, None),
    )
    return jax.shard_map(
        per_device, mesh=mesh, in_specs=in_specs, out_specs=out_specs, check_vma=False
    )
```

```python
import jax
import jax.numpy as jnp
from jax import lax
from jax.experimental import pallas as pl
from jax.experimental.pallas import tpu as pltpu
from jax.sharding import PartitionSpec as P

BLK = 128
F32 = jnp.float32
BF16 = jnp.bfloat16
GROUP = 64
VMEM_BYTES = 20 * 2**20


def call(kernel, scalars, arrays, outs, scratch=(), name=None, far=(), far_outs=()):
    arrays = [
        pltpu.with_memory_space_constraint(array, pltpu.HBM) if i in far else array
        for i, array in enumerate(arrays)
    ]
    in_specs = [pl.BlockSpec(memory_space=pltpu.SMEM) for _ in scalars]
    in_specs += [
        pl.BlockSpec(memory_space=pltpu.HBM if i in far else pltpu.VMEM)
        for i in range(len(arrays))
    ]
    return pl.pallas_call(
        kernel,
        out_shape=[
            pltpu.HBM(*out) if i in far_outs else jax.ShapeDtypeStruct(*out)
            for i, out in enumerate(outs)
        ],
        in_specs=in_specs,
        out_specs=[
            pl.BlockSpec(memory_space=pltpu.HBM if i in far_outs else pltpu.VMEM)
            for i in range(len(outs))
        ],
        scratch_shapes=list(scratch),
        compiler_params=pltpu.CompilerParams(vmem_limit_bytes=VMEM_BYTES),
        name=name,
    )(*scalars, *arrays)


def at(index, size):
    return pl.ds(pl.multiple_of(index * size, size), size)


def dot(left, right, left_dim, right_dim):
    return lax.dot_general(
        left, right, (((left_dim,), (right_dim,)), ((), ())), preferred_element_type=F32
    )


def spread_kernel(tokens, grads, out):
    width = tokens.shape[1]
    out[:, :, :width] = jnp.broadcast_to(tokens[...][None], (out.shape[0],) + tokens.shape)
    out[:, :, width:] = jnp.broadcast_to(grads[...][None], (out.shape[0],) + grads.shape)


def place_kernel(
    slots, gate_blk, up_blk, down_blk, gate_ref, up_out, down_out, up_ref, down_ref, sems
):
    tiles = ((down_blk, down_ref, 2), (up_blk, up_ref, 1), (gate_blk, gate_ref, 0))
    copies = {
        1: pltpu.make_async_copy(up_ref, up_out, sems.at[0]),
        2: pltpu.make_async_copy(down_ref, down_out, sems.at[1]),
    }
    for blk, ref, which in tiles:
        ref[...] = jnp.zeros_like(ref)
        col_blocks = ref.shape[1] // BLK
        total = (ref.shape[0] // BLK) * col_blocks
        for slot in range(blk.shape[0]):
            number = slots[which, slot]

            @pl.when(number < total)
            def _(number=number, slot=slot, blk=blk, ref=ref, col_blocks=col_blocks):
                ref[at(number // col_blocks, BLK), at(number % col_blocks, BLK)] = blk[slot]

        if which > 0:
            copies[which].start()
    copies[1].wait()
    copies[2].wait()


def partial_kernel(panel, gate_w, up_far, down_far, *refs):
    outs, (up_w, down_w, blocks_v, sems, done) = refs[:-5], refs[-5:]
    copies = {
        1: pltpu.make_async_copy(up_far, up_w, sems.at[0]),
        2: pltpu.make_async_copy(down_far, down_w, sems.at[1]),
    }
    copies[1].start()
    copies[2].start()
    width, hid = gate_w.shape
    blocks = hid // BLK
    jobs = ((0, gate_w, 0), (0, up_w, 0), (width, down_w, 1))
    each = len(outs) // 3
    stores = []
    for which, (lo, weight, dim) in enumerate(jobs):
        if which > 0:
            copies[which].wait()
        term = dot(panel[:, lo : lo + width], weight[...], 1, dim).astype(BF16)
        for i in range(each):
            row, col = (i // blocks) * GROUP, (i % blocks) * BLK
            blocks_v[which * each + i] = term[row : row + GROUP, col : col + BLK]
            stores.append(
                pltpu.make_async_copy(
                    blocks_v.at[which * each + i],
                    outs[which * each + i],
                    done.at[which * each + i],
                )
            )
            stores[-1].start()
    for store in stores:
        store.wait()


def output_kernel(gate_w, up_far, down_far, *refs):
    sums, (panel_out, out, panel, up_w, down_w, sems) = refs[:-6], refs[-6:]
    load_up = pltpu.make_async_copy(up_far, up_w, sems.at[0])
    load = pltpu.make_async_copy(down_far, down_w, sems.at[1])
    store = pltpu.make_async_copy(panel, panel_out, sems.at[2])
    load_up.start()
    load.start()
    width, hid = gate_w.shape
    blocks = hid // BLK
    each = len(sums) // 3
    for i in range(each):
        gate, up, cot = (sums[k * each + i][...].astype(F32) for k in range(3))
        sig = jax.nn.sigmoid(gate)
        act = gate * sig
        rows = slice((i // blocks) * GROUP, (i // blocks + 1) * GROUP)
        col = (i % blocks) * BLK
        panel[rows, col : col + BLK] = (act * up).astype(BF16)
        panel[rows, hid + col : hid + col + BLK] = (
            cot * up * (sig * (1.0 + gate * (1.0 - sig)))
        ).astype(BF16)
        panel[rows, 2 * hid + col : 2 * hid + col + BLK] = (cot * act).astype(BF16)
    store.start()
    load_up.wait()
    out[:, width:] = (
        dot(panel[:, hid : 2 * hid], gate_w[...], 1, 1)
        + dot(panel[:, 2 * hid :], up_w[...], 1, 1)
    ).astype(BF16)
    load.wait()
    out[:, :width] = dot(panel[:, :hid], down_w[...], 1, 0).astype(BF16)
    store.wait()


def grad_kernel(slots, panel, hidden, gate_out, up_out, down_out, act_t, hid_t):
    width = panel.shape[1] // 2
    hid = hidden.shape[1] // 3
    for blk in range(width // BLK):
        act_t[blk] = panel[:, blk * BLK : (blk + 1) * BLK].T
    for blk in range(hid // BLK):
        hid_t[blk] = hidden[:, blk * BLK : (blk + 1) * BLK].T
    jobs = (
        (act_t, hidden, hid, hid // BLK, gate_out),
        (act_t, hidden, 2 * hid, hid // BLK, up_out),
        (hid_t, panel, width, width // BLK, down_out),
    )
    for which, (left, right, base, col_blocks, out) in enumerate(jobs):
        total = left.shape[0] * col_blocks
        for slot in range(out.shape[0]):
            number = slots[which, slot]
            live = number < total

            @pl.when(live)
            def _(number=number, slot=slot, left=left, right=right, base=base, out=out, n=col_blocks):
                cols = at(base // BLK + number % n, BLK)
                out[slot] = dot(left[number // n], right[:, cols], 1, 0)

            @pl.when(jnp.logical_not(live))
            def _(slot=slot, out=out):
                out[slot] = jnp.zeros(out.shape[1:], F32)


def sum_kernel(parts, first, second):
    total = jnp.sum(parts[...].astype(F32), axis=0).astype(BF16)
    first[...] = total[:, : first.shape[1]]
    second[...] = total[:, first.shape[1] :]


def per_device(
    tokens, gate_blocks, up_blocks, down_blocks, gate_slots, up_slots, down_slots, out_grad
):
    n_row = lax.axis_size("row")
    local, width = tokens.shape
    count = local * n_row
    hid = 8 * BLK
    wide = 3 * hid
    slots = jnp.stack([gate_slots[0, 0], up_slots[0, 0], down_slots[0, 0]])

    gate_w, up_w, down_w = call(
        place_kernel,
        (slots,),
        (gate_blocks[0, 0], up_blocks[0, 0], down_blocks[0, 0]),
        (((width, hid), BF16), ((width, hid), BF16), ((hid, width), BF16)),
        (
            pltpu.VMEM((width, hid), BF16),
            pltpu.VMEM((hid, width), BF16),
            pltpu.SemaphoreType.DMA((2,)),
        ),
        name="place",
        far_outs=(1, 2),
    )
    (spread,) = call(
        spread_kernel, (), (tokens, out_grad), (((n_row, local, 2 * width), BF16),), name="spread"
    )
    panel = lax.all_to_all(spread, "row", 0, 0, tiled=True).reshape(count, 2 * width)

    n_blocks = 3 * (count // GROUP) * (hid // BLK)
    terms = call(
        partial_kernel,
        (),
        (panel, gate_w, up_w, down_w),
        (((GROUP, BLK), BF16),) * n_blocks,
        (
            pltpu.VMEM((width, hid), BF16),
            pltpu.VMEM((hid, width), BF16),
            pltpu.VMEM((n_blocks, GROUP, BLK), BF16),
            pltpu.SemaphoreType.DMA((2,)),
            pltpu.SemaphoreType.DMA((n_blocks,)),
        ),
        name="partials",
        far=(2, 3),
        far_outs=tuple(range(n_blocks)),
    )
    sums = lax.psum(tuple(terms), "col")
    hidden, out_terms = call(
        output_kernel,
        (),
        (gate_w, up_w, down_w) + tuple(sums),
        (((count, wide), BF16), ((count, 2 * width), BF16)),
        (
            pltpu.VMEM((count, wide), BF16),
            pltpu.VMEM((width, hid), BF16),
            pltpu.VMEM((hid, width), BF16),
            pltpu.SemaphoreType.DMA((3,)),
        ),
        name="outputs",
        far=(1, 2),
        far_outs=(0,),
    )
    parts = lax.all_to_all(
        out_terms.reshape(n_row, local, 2 * width), "row", 0, 0, tiled=True
    )
    gate_grad, up_grad, down_grad = call(
        grad_kernel,
        (slots,),
        (panel, hidden),
        tuple((ref.shape[2:], F32) for ref in (gate_blocks, up_blocks, down_blocks)),
        (
            pltpu.VMEM((width // BLK, BLK, count), BF16),
            pltpu.VMEM((hid // BLK, BLK, count), BF16),
        ),
        name="grads",
    )
    layer_out, token_grad = call(
        sum_kernel, (), (parts,), (((local, width), BF16),) * 2, name="row_sum"
    )
    return (
        layer_out,
        token_grad,
        gate_grad[None, None],
        up_grad[None, None],
        down_grad[None, None],
    )


def solution(mesh):
    in_specs = (
        P("row", "col"),
        P("col", "row", None, None, None),
        P("col", "row", None, None, None),
        P("row", "col", None, None, None),
        P("col", "row", None),
        P("col", "row", None),
        P("row", "col", None),
        P("row", "col"),
    )
    out_specs = (
        P("row", "col"),
        P("row", "col"),
        P("col", "row", None, None, None),
        P("col", "row", None, None, None),
        P("row", "col", None, None, None),
    )
    return jax.shard_map(
        per_device, mesh=mesh, in_specs=in_specs, out_specs=out_specs, check_vma=False
    )
```

```python
import jax
import jax.numpy as jnp
from jax import lax
from jax.experimental import pallas as pl
from jax.experimental.pallas import tpu as pltpu
from jax.sharding import PartitionSpec as P

BLK = 128
F32 = jnp.float32
BF16 = jnp.bfloat16
GROUP = 64
CHUNK = 256
VMEM_BYTES = 20 * 2**20


def call(kernel, scalars, arrays, outs, scratch=(), name=None, far=(), far_outs=()):
    arrays = [
        pltpu.with_memory_space_constraint(array, pltpu.HBM) if i in far else array
        for i, array in enumerate(arrays)
    ]
    in_specs = [pl.BlockSpec(memory_space=pltpu.SMEM) for _ in scalars]
    in_specs += [
        pl.BlockSpec(memory_space=pltpu.HBM if i in far else pltpu.VMEM)
        for i in range(len(arrays))
    ]
    return pl.pallas_call(
        kernel,
        out_shape=[
            pltpu.HBM(*out) if i in far_outs else jax.ShapeDtypeStruct(*out)
            for i, out in enumerate(outs)
        ],
        in_specs=in_specs,
        out_specs=[
            pl.BlockSpec(memory_space=pltpu.HBM if i in far_outs else pltpu.VMEM)
            for i in range(len(outs))
        ],
        scratch_shapes=list(scratch),
        compiler_params=pltpu.CompilerParams(vmem_limit_bytes=VMEM_BYTES),
        name=name,
    )(*scalars, *arrays)


def at(index, size):
    return pl.ds(pl.multiple_of(index * size, size), size)


def dot(left, right, left_dim, right_dim):
    return lax.dot_general(
        left, right, (((left_dim,), (right_dim,)), ((), ())), preferred_element_type=F32
    )


def spread_kernel(tokens, grads, out, sems):
    width = tokens.shape[1]
    copies = []
    for row in range(out.shape[0]):
        for half, source in enumerate((tokens, grads)):
            copies.append(
                pltpu.make_async_copy(
                    source,
                    out.at[row, :, half * width : (half + 1) * width],
                    sems.at[row, half],
                )
            )
            copies[-1].start()
    for copy in copies:
        copy.wait()


def place_kernel(
    slots, gate_blk, up_blk, down_blk, gate_ref, up_out, down_t_out, gate_t_out, up_t_out, down_out,
    up_ref, down_t, gate_t, up_t, down_ref, sems,
):
    jobs = (
        (2, down_blk, down_t, True, down_t_out, 4),
        (1, up_blk, up_ref, False, up_out, 8),
        (0, gate_blk, gate_ref, False, None, 8),
        (0, gate_blk, gate_t, True, gate_t_out, 8),
        (1, up_blk, up_t, True, up_t_out, 8),
        (2, down_blk, down_ref, False, down_out, 4),
    )
    copies = []
    for job, (which, blk, ref, flip, out, col_blocks) in enumerate(jobs):
        ref[...] = jnp.zeros_like(ref)
        total = (ref.shape[0] // BLK) * (ref.shape[1] // BLK)
        for slot in range(blk.shape[0]):
            number = slots[which, slot]

            @pl.when(number < total)
            def _(number=number, slot=slot, blk=blk, ref=ref, flip=flip, n=col_blocks):
                row, col = number // n, number % n
                if flip:
                    ref[at(col, BLK), at(row, BLK)] = blk[slot].T
                else:
                    ref[at(row, BLK), at(col, BLK)] = blk[slot]

        if out is not None:
            copies.append(pltpu.make_async_copy(ref, out, sems.at[job]))
            copies[-1].start()
    for copy in copies:
        copy.wait()


def partial_kernel(panel, gate_w, up_far, down_far, *refs):
    outs, (up_w, down_t, blocks_v, sems, done) = refs[:-5], refs[-5:]
    copies = {
        1: pltpu.make_async_copy(up_far, up_w, sems.at[0]),
        2: pltpu.make_async_copy(down_far, down_t, sems.at[1]),
    }
    copies[1].start()
    copies[2].start()
    width, hid = gate_w.shape
    groups = panel.shape[0] // GROUP
    stores = []
    for which, (lo, weight) in enumerate(((0, gate_w), (0, up_w), (width, down_t))):
        if which > 0:
            copies[which].wait()
        for chunk in range(hid // CHUNK):
            cols = slice(chunk * CHUNK, (chunk + 1) * CHUNK)
            term = dot(panel[:, lo : lo + width], weight[:, cols], 1, 0).astype(BF16)
            for row in range(groups):
                for col in range(CHUNK // BLK):
                    i = len(stores)
                    blocks_v[i] = term[
                        row * GROUP : (row + 1) * GROUP, col * BLK : (col + 1) * BLK
                    ]
                    stores.append(pltpu.make_async_copy(blocks_v.at[i], outs[i], done.at[i]))
                    stores[-1].start()
    for store in stores:
        store.wait()


def output_kernel(gate_far, up_far, down_far, *refs):
    sums, (panel_out, out, panel, gate_t, up_t, down_w, sems) = refs[:-7], refs[-7:]
    loads = [
        pltpu.make_async_copy(far, near, sems.at[i])
        for i, (far, near) in enumerate(((gate_far, gate_t), (up_far, up_t), (down_far, down_w)))
    ]
    store = pltpu.make_async_copy(panel, panel_out, sems.at[3])
    for load in loads:
        load.start()
    hid, width = gate_t.shape
    groups = panel.shape[0] // GROUP
    each = len(sums) // 3
    i = 0
    for chunk in range(hid // CHUNK):
        for row in range(groups):
            for blk in range(CHUNK // BLK):
                gate, up, cot = (sums[k * each + i][...].astype(F32) for k in range(3))
                i += 1
                sig = jax.nn.sigmoid(gate)
                act = gate * sig
                rows = slice(row * GROUP, (row + 1) * GROUP)
                col = chunk * CHUNK + blk * BLK
                panel[rows, col : col + BLK] = (act * up).astype(BF16)
                panel[rows, hid + col : hid + col + BLK] = (
                    cot * up * (sig * (1.0 + gate * (1.0 - sig)))
                ).astype(BF16)
                panel[rows, 2 * hid + col : 2 * hid + col + BLK] = (cot * act).astype(BF16)
    store.start()
    for load in loads:
        load.wait()
    out[:, width:] = (
        dot(panel[:, hid : 2 * hid], gate_t[...], 1, 0)
        + dot(panel[:, 2 * hid :], up_t[...], 1, 0)
    ).astype(BF16)
    out[:, :width] = dot(panel[:, :hid], down_w[...], 1, 0).astype(BF16)
    store.wait()


def grad_kernel(slots, panel, hidden, gate_out, up_out, down_out, act_t, hid_t):
    width = panel.shape[1] // 2
    hid = hidden.shape[1] // 3
    for blk in range(width // BLK):
        act_t[blk] = panel[:, blk * BLK : (blk + 1) * BLK].T
    for blk in range(hid // BLK):
        hid_t[blk] = hidden[:, blk * BLK : (blk + 1) * BLK].T
    jobs = (
        (act_t, hidden, hid, hid // BLK, gate_out),
        (act_t, hidden, 2 * hid, hid // BLK, up_out),
        (hid_t, panel, width, width // BLK, down_out),
    )
    for which, (left, right, base, col_blocks, out) in enumerate(jobs):
        total = left.shape[0] * col_blocks
        for slot in range(out.shape[0]):
            number = slots[which, slot]
            live = number < total

            @pl.when(live)
            def _(number=number, slot=slot, left=left, right=right, base=base, out=out, n=col_blocks):
                cols = at(base // BLK + number % n, BLK)
                out[slot] = dot(left[number // n], right[:, cols], 1, 0)

            @pl.when(jnp.logical_not(live))
            def _(slot=slot, out=out):
                out[slot] = jnp.zeros(out.shape[1:], F32)


def sum_kernel(parts, first, second):
    total = jnp.sum(parts[...].astype(F32), axis=0).astype(BF16)
    first[...] = total[:, : first.shape[1]]
    second[...] = total[:, first.shape[1] :]


def per_device(
    tokens, gate_blocks, up_blocks, down_blocks, gate_slots, up_slots, down_slots, out_grad
):
    n_row = lax.axis_size("row")
    local, width = tokens.shape
    count = local * n_row
    hid = 8 * BLK
    wide = 3 * hid
    slots = jnp.stack([gate_slots[0, 0], up_slots[0, 0], down_slots[0, 0]])

    gate_w, up_w, down_t, gate_t, up_t, down_w = call(
        place_kernel,
        (slots,),
        (gate_blocks[0, 0], up_blocks[0, 0], down_blocks[0, 0]),
        tuple((shape, BF16) for shape in ((width, hid),) * 3 + ((hid, width),) * 3),
        (
            pltpu.VMEM((width, hid), BF16),
            pltpu.VMEM((width, hid), BF16),
            pltpu.VMEM((hid, width), BF16),
            pltpu.VMEM((hid, width), BF16),
            pltpu.VMEM((hid, width), BF16),
            pltpu.SemaphoreType.DMA((6,)),
        ),
        name="place",
        far_outs=(1, 2, 3, 4, 5),
    )
    (spread,) = call(
        spread_kernel,
        (),
        (tokens, out_grad),
        (((n_row, local, 2 * width), BF16),),
        (pltpu.SemaphoreType.DMA((n_row, 2)),),
        name="spread",
        far=(0, 1),
        far_outs=(0,),
    )
    panel = lax.all_to_all(spread, "row", 0, 0, tiled=True).reshape(count, 2 * width)

    n_blocks = 3 * (count // GROUP) * (hid // BLK)
    terms = call(
        partial_kernel,
        (),
        (panel, gate_w, up_w, down_t),
        (((GROUP, BLK), BF16),) * n_blocks,
        (
            pltpu.VMEM((width, hid), BF16),
            pltpu.VMEM((width, hid), BF16),
            pltpu.VMEM((n_blocks, GROUP, BLK), BF16),
            pltpu.SemaphoreType.DMA((2,)),
            pltpu.SemaphoreType.DMA((n_blocks,)),
        ),
        name="partials",
        far=(2, 3),
        far_outs=tuple(range(n_blocks)),
    )
    sums = lax.psum(tuple(terms), "col")
    hidden, out_terms = call(
        output_kernel,
        (),
        (gate_t, up_t, down_w) + tuple(sums),
        (((count, wide), BF16), ((count, 2 * width), BF16)),
        (
            pltpu.VMEM((count, wide), BF16),
            pltpu.VMEM((hid, width), BF16),
            pltpu.VMEM((hid, width), BF16),
            pltpu.VMEM((hid, width), BF16),
            pltpu.SemaphoreType.DMA((4,)),
        ),
        name="outputs",
        far=(0, 1, 2),
        far_outs=(0,),
    )
    parts = lax.all_to_all(
        out_terms.reshape(n_row, local, 2 * width), "row", 0, 0, tiled=True
    )
    gate_grad, up_grad, down_grad = call(
        grad_kernel,
        (slots,),
        (panel, hidden),
        tuple((ref.shape[2:], F32) for ref in (gate_blocks, up_blocks, down_blocks)),
        (
            pltpu.VMEM((width // BLK, BLK, count), BF16),
            pltpu.VMEM((hid // BLK, BLK, count), BF16),
        ),
        name="grads",
    )
    layer_out, token_grad = call(
        sum_kernel, (), (parts,), (((local, width), BF16),) * 2, name="row_sum"
    )
    return (
        layer_out,
        token_grad,
        gate_grad[None, None],
        up_grad[None, None],
        down_grad[None, None],
    )


def solution(mesh):
    in_specs = (
        P("row", "col"),
        P("col", "row", None, None, None),
        P("col", "row", None, None, None),
        P("row", "col", None, None, None),
        P("col", "row", None),
        P("col", "row", None),
        P("row", "col", None),
        P("row", "col"),
    )
    out_specs = (
        P("row", "col"),
        P("row", "col"),
        P("col", "row", None, None, None),
        P("col", "row", None, None, None),
        P("row", "col", None, None, None),
    )
    return jax.shard_map(
        per_device, mesh=mesh, in_specs=in_specs, out_specs=out_specs, check_vma=False
    )
```

```python
import jax
import jax.numpy as jnp
from jax import lax
from jax.experimental import pallas as pl
from jax.experimental.pallas import tpu as pltpu
from jax.sharding import PartitionSpec as P

BLK = 128
F32 = jnp.float32
BF16 = jnp.bfloat16
GROUP = 64
VMEM_BYTES = 20 * 2**20


def call(kernel, scalars, arrays, outs, scratch=(), name=None, far=(), far_outs=()):
    arrays = [
        pltpu.with_memory_space_constraint(array, pltpu.HBM) if i in far else array
        for i, array in enumerate(arrays)
    ]
    in_specs = [pl.BlockSpec(memory_space=pltpu.SMEM) for _ in scalars]
    in_specs += [
        pl.BlockSpec(memory_space=pltpu.HBM if i in far else pltpu.VMEM)
        for i in range(len(arrays))
    ]
    return pl.pallas_call(
        kernel,
        out_shape=[
            pltpu.HBM(*out) if i in far_outs else jax.ShapeDtypeStruct(*out)
            for i, out in enumerate(outs)
        ],
        in_specs=in_specs,
        out_specs=[
            pl.BlockSpec(memory_space=pltpu.HBM if i in far_outs else pltpu.VMEM)
            for i in range(len(outs))
        ],
        scratch_shapes=list(scratch),
        compiler_params=pltpu.CompilerParams(vmem_limit_bytes=VMEM_BYTES),
        name=name,
    )(*scalars, *arrays)


def at(index, size):
    return pl.ds(pl.multiple_of(index * size, size), size)


def dot(left, right, left_dim, right_dim):
    return lax.dot_general(
        left, right, (((left_dim,), (right_dim,)), ((), ())), preferred_element_type=F32
    )


def spread_kernel(tokens, grads, out, near, sems):
    width = tokens.shape[1]
    copies = [
        pltpu.make_async_copy(tokens, near.at[0], sems.at[0]),
        pltpu.make_async_copy(grads, near.at[1], sems.at[1]),
    ]
    for copy in copies:
        copy.start()
    for half, copy in enumerate(copies):
        copy.wait()
        out[:, :, half * width : (half + 1) * width] = jnp.broadcast_to(
            near[half][None], (out.shape[0],) + tokens.shape
        )


def place_kernel(
    slots, gate_blk, up_blk, down_blk, gate_out, up_out, down_out, gate_ref, up_ref, down_ref, sems
):
    tiles = (
        (gate_blk, gate_ref, gate_out),
        (up_blk, up_ref, up_out),
        (down_blk, down_ref, down_out),
    )
    copies = []
    for which, (blk, ref, out) in enumerate(tiles):
        ref[...] = jnp.zeros_like(ref)
        col_blocks = ref.shape[1] // BLK
        total = (ref.shape[0] // BLK) * col_blocks
        for slot in range(blk.shape[0]):
            number = slots[which, slot]

            @pl.when(number < total)
            def _(number=number, slot=slot, blk=blk, ref=ref, col_blocks=col_blocks):
                ref[at(number // col_blocks, BLK), at(number % col_blocks, BLK)] = blk[slot]

        copies.append(pltpu.make_async_copy(ref, out, sems.at[which]))
        copies[-1].start()
    for copy in copies:
        copy.wait()


def partial_kernel(panel, gate_far, up_far, down_far, panel_out, *refs):
    outs, (gate_w, up_w, down_w, sems) = refs[:-4], refs[-4:]
    pairs = ((gate_far, gate_w), (up_far, up_w), (down_far, down_w))
    loads = [pltpu.make_async_copy(far, near, sems.at[i]) for i, (far, near) in enumerate(pairs)]
    for load in loads:
        load.start()
    keep = pltpu.make_async_copy(panel, panel_out, sems.at[3])
    keep.start()
    width, hid = gate_w.shape
    blocks = hid // BLK
    jobs = ((0, gate_w, 0), (0, up_w, 0), (width, down_w, 1))
    each = len(outs) // 3
    for which, (lo, weight, dim) in enumerate(jobs):
        loads[which].wait()
        term = dot(panel[:, lo : lo + width], weight[...], 1, dim).astype(BF16)
        for i in range(each):
            row, col = (i // blocks) * GROUP, (i % blocks) * BLK
            outs[which * each + i][...] = term[row : row + GROUP, col : col + BLK]
    keep.wait()


def output_kernel(gate_far, up_far, down_far, *refs):
    sums, (panel_out, out, panel, gate_w, up_w, down_w, sems) = refs[:-7], refs[-7:]
    load_gate = pltpu.make_async_copy(gate_far, gate_w, sems.at[3])
    load_gate.start()
    load_up = pltpu.make_async_copy(up_far, up_w, sems.at[0])
    load = pltpu.make_async_copy(down_far, down_w, sems.at[1])
    store = pltpu.make_async_copy(panel, panel_out, sems.at[2])
    load_up.start()
    load.start()
    width, hid = gate_w.shape
    blocks = hid // BLK
    each = len(sums) // 3
    for i in range(each):
        gate, up, cot = (sums[k * each + i][...].astype(F32) for k in range(3))
        sig = jax.nn.sigmoid(gate)
        act = gate * sig
        rows = slice((i // blocks) * GROUP, (i // blocks + 1) * GROUP)
        col = (i % blocks) * BLK
        panel[rows, col : col + BLK] = (act * up).astype(BF16)
        panel[rows, hid + col : hid + col + BLK] = (
            cot * up * (sig * (1.0 + gate * (1.0 - sig)))
        ).astype(BF16)
        panel[rows, 2 * hid + col : 2 * hid + col + BLK] = (cot * act).astype(BF16)
    store.start()
    load_gate.wait()
    load_up.wait()
    out[:, width:] = (
        dot(panel[:, hid : 2 * hid], gate_w[...], 1, 1)
        + dot(panel[:, 2 * hid :], up_w[...], 1, 1)
    ).astype(BF16)
    load.wait()
    out[:, :width] = dot(panel[:, :hid], down_w[...], 1, 0).astype(BF16)
    store.wait()


def grad_kernel(slots, panel, hidden, gate_out, up_out, down_out, act_t, hid_t):
    width = panel.shape[1] // 2
    hid = hidden.shape[1] // 3
    for blk in range(width // BLK):
        act_t[blk] = panel[:, blk * BLK : (blk + 1) * BLK].T
    for blk in range(hid // BLK):
        hid_t[blk] = hidden[:, blk * BLK : (blk + 1) * BLK].T
    jobs = (
        (act_t, hidden, hid, hid // BLK, gate_out),
        (act_t, hidden, 2 * hid, hid // BLK, up_out),
        (hid_t, panel, width, width // BLK, down_out),
    )
    for which, (left, right, base, col_blocks, out) in enumerate(jobs):
        total = left.shape[0] * col_blocks
        for slot in range(out.shape[0]):
            number = slots[which, slot]
            live = number < total

            @pl.when(live)
            def _(number=number, slot=slot, left=left, right=right, base=base, out=out, n=col_blocks):
                cols = at(base // BLK + number % n, BLK)
                out[slot] = dot(left[number // n], right[:, cols], 1, 0)

            @pl.when(jnp.logical_not(live))
            def _(slot=slot, out=out):
                out[slot] = jnp.zeros(out.shape[1:], F32)


def sum_kernel(parts, first, second):
    total = jnp.sum(parts[...].astype(F32), axis=0).astype(BF16)
    first[...] = total[:, : first.shape[1]]
    second[...] = total[:, first.shape[1] :]


def per_device(
    tokens, gate_blocks, up_blocks, down_blocks, gate_slots, up_slots, down_slots, out_grad
):
    n_row = lax.axis_size("row")
    local, width = tokens.shape
    count = local * n_row
    hid = 8 * BLK
    wide = 3 * hid
    slots = jnp.stack([gate_slots[0, 0], up_slots[0, 0], down_slots[0, 0]])

    gate_w, up_w, down_w = call(
        place_kernel,
        (slots,),
        (gate_blocks[0, 0], up_blocks[0, 0], down_blocks[0, 0]),
        (((width, hid), BF16), ((width, hid), BF16), ((hid, width), BF16)),
        (
            pltpu.VMEM((width, hid), BF16),
            pltpu.VMEM((width, hid), BF16),
            pltpu.VMEM((hid, width), BF16),
            pltpu.SemaphoreType.DMA((3,)),
        ),
        name="place",
        far_outs=(0, 1, 2),
    )
    (spread,) = call(
        spread_kernel,
        (),
        (tokens, out_grad),
        (((n_row, local, 2 * width), BF16),),
        (pltpu.VMEM((2, local, width), BF16), pltpu.SemaphoreType.DMA((2,))),
        name="spread",
        far=(0, 1),
    )
    panel = lax.all_to_all(spread, "row", 0, 0, tiled=True).reshape(count, 2 * width)

    n_blocks = 3 * (count // GROUP) * (hid // BLK)
    kept, *terms = call(
        partial_kernel,
        (),
        (panel, gate_w, up_w, down_w),
        (((count, 2 * width), BF16),) + (((GROUP, BLK), BF16),) * n_blocks,
        (
            pltpu.VMEM((width, hid), BF16),
            pltpu.VMEM((width, hid), BF16),
            pltpu.VMEM((hid, width), BF16),
            pltpu.SemaphoreType.DMA((4,)),
        ),
        name="partials",
        far=(1, 2, 3),
        far_outs=(0,),
    )
    sums = lax.psum(tuple(terms), "col")
    hidden, out_terms = call(
        output_kernel,
        (),
        (gate_w, up_w, down_w) + tuple(sums),
        (((count, wide), BF16), ((count, 2 * width), BF16)),
        (
            pltpu.VMEM((count, wide), BF16),
            pltpu.VMEM((width, hid), BF16),
            pltpu.VMEM((width, hid), BF16),
            pltpu.VMEM((hid, width), BF16),
            pltpu.SemaphoreType.DMA((4,)),
        ),
        name="outputs",
        far=(0, 1, 2),
        far_outs=(0,),
    )
    parts = lax.all_to_all(
        out_terms.reshape(n_row, local, 2 * width), "row", 0, 0, tiled=True
    )
    gate_grad, up_grad, down_grad = call(
        grad_kernel,
        (slots,),
        (kept, hidden),
        tuple((ref.shape[2:], F32) for ref in (gate_blocks, up_blocks, down_blocks)),
        (
            pltpu.VMEM((width // BLK, BLK, count), BF16),
            pltpu.VMEM((hid // BLK, BLK, count), BF16),
        ),
        name="grads",
    )
    layer_out, token_grad = call(
        sum_kernel, (), (parts,), (((local, width), BF16),) * 2, name="row_sum"
    )
    return (
        layer_out,
        token_grad,
        gate_grad[None, None],
        up_grad[None, None],
        down_grad[None, None],
    )


def solution(mesh):
    in_specs = (
        P("row", "col"),
        P("col", "row", None, None, None),
        P("col", "row", None, None, None),
        P("row", "col", None, None, None),
        P("col", "row", None),
        P("col", "row", None),
        P("row", "col", None),
        P("row", "col"),
    )
    out_specs = (
        P("row", "col"),
        P("row", "col"),
        P("col", "row", None, None, None),
        P("col", "row", None, None, None),
        P("row", "col", None, None, None),
    )
    return jax.shard_map(
        per_device, mesh=mesh, in_specs=in_specs, out_specs=out_specs, check_vma=False
    )
```
